32 devices in a mesh: dp: 8 (over y, x, core), expert: 4 (over z).
Axes of the slice: x: 2, y: 2, z: 4, core: 2. Of those that a mesh axis runs over, the one named last changes fastest.
Arguments:
- tokens: bfloat16 [8192, 2048], P(('dp', 'expert')), may hold values from -6 to 6
- cotangent: bfloat16 [8192, 2048], P(('dp', 'expert')), may hold values from -6 to 6
- routes: int32 [8192, 2], P(('dp', 'expert')), may hold values from 0 to 3, all different within a row; in each aligned block of 256 rows (0 to 255, 256 to 511, ...) at most 192 rows name the same one
- gate_probs: float32 [8192, 2], P(('dp', 'expert')), may hold values from 0.2 to 1
- w_up: bfloat16 [4, 2048, 768], P('expert'), may hold values from -0.125 to 0.125
- w_down: bfloat16 [4, 768, 2048], P('expert'), may hold values from -0.21875 to 0.21875
- decay_rate: float32 [4, 768], P('expert'), may hold values from 0.3 to 0.95
Outputs:
- layer_out: bfloat16 [8192, 2048], P(('dp', 'expert'))
- token_grad: bfloat16 [8192, 2048], P(('dp', 'expert'))
- gate_grad: float32 [8192, 2], P(('dp', 'expert'))
- up_grad: float32 [4, 2048, 768], P('expert', 'dp')
- down_grad: float32 [4, 768, 2048], P('expert', None, 'dp')
The draws below stay inside these ranges and needn't reach their ends.
Inputs may be any that keep to these rules, and one draw needn't show every extreme that they name: `routes`: each token names two different experts; among the 256 rows of one device no expert is named by more than 192 rows, and in every draw some expert is named by exactly 192 rows of some device.
All inputs are finite; a program needn't handle non-finite values.
Results may differ from the reference program's by a relative error of at most 0.015.
Values may be sent and summed in bfloat16 or wider, within the bound.
A program may use at most 128 MiB of HBM per device.

```python
import math
from functools import partial
import jax
import jax.numpy as jnp
import numpy as np
from jax import lax

D = 2048
FF = 768
STEPS = 4
TOK_DEV = 256
EXPERTS = 4
CAP = 192
TOKENS = 8192


def strengthened(array, key, source, target, shards_of, factor):
    owner, partner = [(jnp.arange(array.shape[dim]) // (array.shape[dim] // shards_of)).reshape([-1 if axis == dim else 1 for axis in range(array.ndim)]) for dim in (source, target)]
    chosen = jax.random.permutation(key, shards_of)[partner]
    strong = (owner == chosen) | (owner == (partner + shards_of // 2) % shards_of)
    return jnp.where(strong, factor * array, array)


def levels(own_key, shape, shards, smallest, largest):
    def one(axis_at, blocks):
        draws = jax.random.uniform(jax.random.fold_in(jax.random.fold_in(own_key, 6), axis_at), (blocks,), jnp.float32, smallest / len(shards), largest / len(shards))
        return jnp.repeat(jnp.exp(draws), shape[axis_at] // blocks).reshape((-1,) + (1,) * (len(shape) - axis_at - 1))

    loudness = one(*shards[0])
    for cut in shards[1:]:
        loudness = loudness * one(*cut)
    return loudness


def deal_out(stream_key, own, number, rows, count, top, limit, skew):
    order = jax.random.permutation(stream_key, count)
    packed, ordinary = load_shares(count, rows * top, limit, skew, True), load_shares(count, rows * top, limit, skew, False)
    places = jnp.arange(count)

    def named(sizes, turn):
        used = int((sizes > 0).sum())
        fixed = max(1, used // 4)
        passed = fixed + (places - fixed + turn * (used - fixed)) % max(1, count - fixed)
        return jnp.zeros((count,), jnp.int32).at[order[jnp.where(places < fixed, places, passed)]].set(jnp.asarray(sizes, jnp.int32))

    sizes = jnp.where(number % 4 == 0, named(packed, number // 4), named(ordinary, number - number // 4 - 1))
    mixed = jax.random.permutation(jax.random.fold_in(own, 3), count)
    source_of, receiver = mixed[0:count // 2 * 2:2], mixed[1:count // 2 * 2:2]
    margin = jnp.minimum(sizes[source_of] - 1, limit - sizes[receiver]) // 2
    margin = jnp.where((source_of == order[0]) | (receiver == order[0]) | (sizes[receiver] == 0), 0, jnp.maximum(margin, 0))
    passed = jax.random.randint(jax.random.fold_in(own, 4), (count // 2,), 0, 1 << 20) % (margin + 1)
    sizes = sizes.at[source_of].add(-passed).at[receiver].add(passed)
    members = jnp.searchsorted(jnp.cumsum(sizes), jnp.arange(rows * top), side="right").astype(jnp.int32)
    listing = members.reshape(top, rows).T
    listing = listing[jax.random.permutation(jax.random.fold_in(own, 1), rows)]
    turn = jax.random.randint(jax.random.fold_in(own, 2), (rows, 1), 0, top)
    return jnp.take_along_axis(listing, (jnp.arange(top)[None, :] + turn) % top, axis=1)


def load_shares(count, total, limit, skew, full):
    portions = [(1 << 20) // math.isqrt(rank ** skew) + 1 for rank in range(1, count + 1)]
    largest = limit if full else min(limit, max(-(-total // count), total * portions[0] // sum(portions)))
    least = 1 if total - largest >= count - 1 else 0
    counts, spare = [largest] + [least] * (count - 1), total - largest - least * (count - 1)
    while spare > 0:
        candidates = [i for i in range(1, count) if counts[i] < largest] or [i for i in range(1, count) if counts[i] < limit]
        whole, remaining = sum([portions[i] for i in candidates]), spare
        for i in candidates:
            more = min(limit - counts[i], max(1, remaining * portions[i] // whole), spare)
            counts[i] = counts[i] + more
            spare = spare - more
    return np.array(counts)


def noise(stream_key, extent, scale, limit, shards=(), kind=jnp.bfloat16):
    drawn = jax.random.normal(stream_key, extent, jnp.float32) * scale
    if len(shards) > 0:
        drawn = levels(stream_key, extent, shards, -0.22, 0.18) * drawn
    return jnp.clip(drawn, min=-limit, max=limit).astype(kind)


def noise_with(key, shape, width, reach, pieces, heavy, kind=jnp.bfloat16):
    array = width * jax.random.normal(key, shape, jnp.float32)
    if pieces:
        array = array * levels(key, shape, pieces, -0.22, 0.18)
    return jnp.clip(strengthened(array, jax.random.fold_in(key, 3), *heavy), -reach, reach).astype(kind)


def setup_inputs(seed: int = 0) -> dict:
    arg_keys = jax.random.split(jax.random.key(seed), 8)
    tokens = noise_with(arg_keys[0], (TOKENS, D), 1.0, 6.0, ((0, 32),), (0, 1, 32, 2.75))
    cotangent = noise_with(arg_keys[1], (TOKENS, D), 1.0, 6.0, ((0, 32),), (0, 1, 32, 2.75))
    routes_keys = jax.random.split(jax.random.fold_in(arg_keys[2], 1), TOKENS // TOK_DEV)
    routes_turns = jax.random.permutation(jax.random.fold_in(arg_keys[2], 3), TOKENS // TOK_DEV)
    routes = jax.vmap(lambda own, number: deal_out(jax.random.fold_in(arg_keys[2], 2), own, number, TOK_DEV, EXPERTS, 2, CAP, 2))(routes_keys, routes_turns).reshape((TOKENS, 2))
    gate_probs = jnp.clip(0.2 + 0.8 * jax.random.uniform(arg_keys[3], (TOKENS, 2), jnp.float32) ** levels(arg_keys[3], (TOKENS, 2), ((0, 32),), -0.2, 0.2), 0.2, 1.0)
    w_up = noise(arg_keys[4], (EXPERTS, D, FF), D ** -0.5, 0.125, ((0, 4),))
    w_down = noise(arg_keys[5], (EXPERTS, FF, D), FF ** -0.5, 0.21875, ((0, 4),))
    decay_rate = jnp.clip(jnp.exp(math.log(0.95) - 1.1526795 * jax.random.uniform(arg_keys[6], (EXPERTS, FF), jnp.float32) ** levels(arg_keys[6], (EXPERTS, FF), ((0, 4),), -0.2, 0.2)), 0.3, 0.95)
    return {"tokens": tokens, "cotangent": cotangent, "routes": routes, "gate_probs": gate_probs, "w_up": w_up, "w_down": w_down, "decay_rate": decay_rate}


sharpness = 4.0

def spike_rate(current, decay_rate):
    potential = jnp.zeros_like(current)
    running = jnp.zeros_like(current)
    for tick_index in range(STEPS):
        potential = decay_rate * potential + current
        spikes = jax.nn.sigmoid(sharpness * (potential - 1.0))
        potential = potential - spikes
        running = running + spikes
    return running / STEPS

def place_slots(route_rows, experts_here, capacity):
    chosen = route_rows.reshape(-1).astype(jnp.int32)
    onehot = (chosen[:, None] == jnp.arange(experts_here, dtype=jnp.int32)[None, :]).astype(jnp.int32)
    rank_table = (jnp.cumsum(onehot, axis=0) - 1).astype(jnp.int32)
    return chosen * capacity + lax.optimization_barrier(jnp.sum(rank_table * onehot, axis=1)).astype(jnp.int32)

def fill_slots(position, slot_count):
    order = jnp.arange(position.shape[0], dtype=jnp.int32)
    slot_owner = jnp.zeros((slot_count,), jnp.int32).at[position].set(order)
    live_slots = jnp.zeros((slot_count,), jnp.int32).at[position].set(1)
    return (slot_owner, live_slots)

def expert_pass(recv_rows, rows_grad, weight_up, weight_down, rates_decay):
    current = jnp.dot(recv_rows, weight_up, preferred_element_type=jnp.float32)
    rates, pullback = jax.vjp(partial(spike_rate, decay_rate=rates_decay), current)
    rates_low = rates.astype(jnp.bfloat16)
    outputs = jnp.dot(rates_low, weight_down, preferred_element_type=jnp.float32).astype(jnp.bfloat16)
    rate_grad = jnp.dot(rows_grad, weight_down.T, preferred_element_type=jnp.float32)
    current_grad = pullback(rate_grad)[0].astype(jnp.bfloat16)
    rows_back = jnp.dot(current_grad, weight_up.T, preferred_element_type=jnp.float32).astype(jnp.bfloat16)
    return (outputs, rows_back, rates_low, current_grad)

def reference(tokens, cotangent, routes, gate_probs, w_up, w_down, decay_rate):
    blocks = TOKENS // TOK_DEV
    slot_count = EXPERTS * CAP
    position = jax.vmap(partial(place_slots, experts_here=EXPERTS, capacity=CAP))(routes.reshape(blocks, TOK_DEV * 2))
    slot_owner, live_slots = jax.vmap(partial(fill_slots, slot_count=slot_count))(position)
    token_blocks = tokens.reshape(blocks, TOK_DEV, D)
    cot_blocks = cotangent.reshape(blocks, TOK_DEV, D)
    gate_blocks = gate_probs.reshape(blocks, TOK_DEV * 2)
    take_rows = jax.vmap(lambda source, index: source[index])

    def one_expert(operands):
        weight_up, weight_down, rates_decay, expert_id = operands
        owners = lax.dynamic_slice_in_dim(slot_owner, expert_id * CAP, CAP, 1)
        live = lax.dynamic_slice_in_dim(live_slots, expert_id * CAP, CAP, 1) > 0
        token_index = owners // 2
        zero = jnp.zeros((), jnp.bfloat16)
        recv_rows = jnp.where(live[:, :, None], take_rows(token_blocks, token_index), zero)
        slot_gates = take_rows(gate_blocks, owners)
        scaled = (slot_gates[:, :, None] * take_rows(cot_blocks, token_index).astype(jnp.float32)).astype(jnp.bfloat16)
        rows_grad = jnp.where(live[:, :, None], scaled, zero)
        flat_rows = recv_rows.reshape(blocks * CAP, D)
        flat_grad = rows_grad.reshape(blocks * CAP, D)
        outputs, rows_back, rates_low, current_grad = expert_pass(flat_rows, flat_grad, weight_up, weight_down, rates_decay)
        grad_up = jnp.dot(flat_rows.T, current_grad, preferred_element_type=jnp.float32)
        grad_down = jnp.dot(rates_low.T, flat_grad, preferred_element_type=jnp.float32)
        return (outputs.reshape(blocks, CAP, D), rows_back.reshape(blocks, CAP, D), grad_up, grad_down)
    expert_ids = jnp.arange(EXPERTS, dtype=jnp.int32)
    expert_out, expert_back, up_grad, down_grad = lax.map(one_expert, (w_up, w_down, decay_rate, expert_ids))
    chosen = routes.reshape(blocks, TOK_DEV * 2).astype(jnp.int32)
    block_ids = jnp.arange(blocks, dtype=jnp.int32)[:, None]
    assign_index = ((chosen * blocks + block_ids) * CAP + (position - chosen * CAP)).reshape(-1)
    flat_out = expert_out.reshape(-1, D)[assign_index].reshape(TOKENS, 2, D).astype(jnp.float32)
    flat_back = expert_back.reshape(-1, D)[assign_index].reshape(TOKENS, 2, D).astype(jnp.float32)
    layer_out = lax.optimization_barrier(jnp.sum(gate_probs[:, :, None] * flat_out, axis=1)).astype(jnp.bfloat16)
    gate_grad = lax.optimization_barrier(jnp.sum(cotangent[:, None, :].astype(jnp.float32) * flat_out, axis=2))
    token_grad = lax.optimization_barrier(jnp.sum(flat_back, axis=1)).astype(jnp.bfloat16)
    return (layer_out, token_grad, gate_grad, up_grad, down_grad)
```

```python
import jax
import jax.numpy as jnp
from jax import lax
from jax.sharding import PartitionSpec as P

STEPS = 4
SHARP = 4.0


BF = jnp.bfloat16
F32 = jnp.float32


def rate_and_slope(current, decay):
    v = jnp.zeros_like(current)
    dv = jnp.zeros_like(current)
    total = jnp.zeros_like(current)
    slope = jnp.zeros_like(current)
    for _ in range(STEPS):
        v = decay * v + current
        dv = decay * dv + 1.0
        s = jax.nn.sigmoid(SHARP * (v - 1.0))
        ds = SHARP * s * (1.0 - s) * dv
        v = v - s
        dv = dv - ds
        total = total + s
        slope = slope + ds
    return total / STEPS, slope / STEPS


def mm(a, b, dims):
    return lax.dot_general(a, b, (dims, ((), ())), preferred_element_type=F32)


def expert_block(x, cot, gate, w_up, w_down, decay):
    rates, slope = rate_and_slope(mm(x, w_up, ((1,), (0,))), decay)
    rates = rates.astype(BF)
    cot32 = cot.astype(F32)
    scaled = (gate[:, None] * cot32).astype(BF)
    out = mm(rates, w_down, ((1,), (0,))).astype(BF).astype(F32)
    layer = gate[:, None] * out
    dots = jnp.sum(cot32 * out, axis=1)
    rate_grad = mm(scaled, w_down, ((1,), (1,)))
    current_grad = (rate_grad * slope).astype(BF)
    back = mm(current_grad, w_up, ((1,), (1,))).astype(BF).astype(F32)
    return layer, dots, back, rates, scaled, current_grad


def local(tokens, cotangent, routes, gate_probs, w_up, w_down, decay_rate):
    rows, width = tokens.shape
    n = lax.axis_size("expert")
    parts = lax.axis_size("dp")
    half = n // 2
    me = lax.axis_index("expert")
    slot = lax.axis_index("dp")
    w_up, w_down, decay = w_up[0], w_down[0], decay_rate[0]
    hidden = w_up.shape[1]

    def swap(x, d):
        return lax.ppermute(x, "expert", [(i, i ^ d) for i in range(n)])

    up_piece = lax.dynamic_slice_in_dim(w_up, slot * (width // parts), width // parts, 0)
    down_piece = lax.dynamic_slice_in_dim(w_down, slot * (hidden // parts), hidden // parts, 0)
    w_up2 = lax.all_gather(swap(up_piece, half), "dp", axis=0, tiled=True)
    w_down2 = lax.all_gather(swap(down_piece, half), "dp", axis=0, tiled=True)
    decay2 = swap(decay, half)

    table = jnp.sum(
        jnp.where(
            routes[:, :, None] == jnp.arange(n, dtype=jnp.int32)[None, None, :],
            gate_probs[:, :, None],
            0.0,
        ),
        axis=1,
    )
    xs = [tokens] + [swap(tokens, d) for d in range(1, half)]
    cots = [cotangent] + [swap(cotangent, d) for d in range(1, half)]
    tables = [table] + [swap(table, d) for d in range(1, half)]

    def gate_of(tab, expert):
        return jnp.sum(
            jnp.where(jnp.arange(n, dtype=jnp.int32)[None, :] == expert, tab, 0.0), axis=1
        )

    x_all = jnp.concatenate(xs, axis=0)
    cot_all = jnp.concatenate(cots, axis=0)
    tab_all = jnp.concatenate(tables, axis=0)
    other = me ^ half

    def scatter(a, b):
        return lax.psum_scatter(
            mm(a, b, ((0,), (0,))).astype(BF), "dp", scatter_dimension=0, tiled=True
        )

    layer1, dots1, back1, rates1, scaled1, cg1 = expert_block(
        x_all, cot_all, gate_of(tab_all, me), w_up, w_down, decay
    )
    up1, down1 = scatter(x_all, cg1), scatter(scaled1, rates1)
    layer2, dots2, back2, rates2, scaled2, cg2 = expert_block(
        x_all, cot_all, gate_of(tab_all, other), w_up2, w_down2, decay2
    )
    up2, down2 = swap(scatter(x_all, cg2), half), swap(scatter(scaled2, rates2), half)
    layer = layer1 + layer2
    back = back1 + back2
    ids = jnp.arange(n, dtype=jnp.int32)[None, :]
    dots = jnp.where(ids == me, dots1[:, None], 0.0) + jnp.where(
        ids == other, dots2[:, None], 0.0
    )
    layer_out, token_grad, dot_own = layer[:rows], back[:rows], dots[:rows]
    for d in range(1, half):
        cut = slice(d * rows, (d + 1) * rows)
        layer_out = layer_out + swap(layer[cut].astype(BF), d).astype(F32)
        token_grad = token_grad + swap(back[cut].astype(BF), d).astype(F32)
        dot_own = dot_own + swap(dots[cut], d)
    gate_grad = jnp.sum(
        jnp.where(
            routes[:, :, None] == jnp.arange(n, dtype=jnp.int32)[None, None, :],
            dot_own[:, None, :],
            0.0,
        ),
        axis=2,
    )
    up_grad = up1.astype(F32) + up2.astype(F32)
    down_grad = down1.astype(F32) + down2.astype(F32)
    return (layer_out.astype(BF), token_grad.astype(BF), gate_grad, up_grad[None], down_grad.T[None])


def solution(mesh):
    rows = P(("dp", "expert"), None)
    return jax.shard_map(
        local,
        mesh=mesh,
        in_specs=(rows, rows, rows, rows, P("expert", None, None), P("expert", None, None), P("expert", None)),
        out_specs=(rows, rows, rows, P("expert", "dp", None), P("expert", None, "dp")),
        check_vma=False,
    )
```

```python
from functools import partial

import jax
import jax.numpy as jnp
from jax import lax
from jax.experimental import pallas as pl
from jax.experimental.pallas import tpu as pltpu
from jax.sharding import PartitionSpec as P

STEPS = 4
SHARP = 4.0

BF = jnp.bfloat16
F32 = jnp.float32


def rate_and_slope(current, decay):
    v = jnp.zeros_like(current)
    dv = jnp.zeros_like(current)
    total = jnp.zeros_like(current)
    slope = jnp.zeros_like(current)
    for _ in range(STEPS):
        v = decay * v + current
        dv = decay * dv + 1.0
        s = jax.nn.sigmoid(SHARP * (v - 1.0))
        ds = SHARP * s * (1.0 - s) * dv
        v = v - s
        dv = dv - ds
        total = total + s
        slope = slope + ds
    return total / STEPS, slope / STEPS


def mm(a, b, dims):
    return lax.dot_general(a, b, (dims, ((), ())), preferred_element_type=F32)


def expert_block(x, cot, gate, w_up, w_down, decay):
    rates, slope = rate_and_slope(mm(x, w_up, ((1,), (0,))), decay)
    rates = rates.astype(BF)
    cot32 = cot.astype(F32)
    scaled = (gate[:, None] * cot32).astype(BF)
    out = mm(rates, w_down, ((1,), (0,))).astype(BF).astype(F32)
    layer = gate[:, None] * out
    dots = jnp.sum(cot32 * out, axis=1)
    rate_grad = mm(scaled, w_down, ((1,), (1,)))
    current_grad = (rate_grad * slope).astype(BF)
    back = mm(current_grad, w_up, ((1,), (1,))).astype(BF).astype(F32)
    return layer, dots, back, rates, scaled, current_grad


def flip(pos, mask):
    for k in range(mask.bit_length()):
        b = 1 << k
        if mask & b:
            pos = pos + b * (1 - 2 * ((pos // b) % 2))
    return pos


def bit_orders(parts):
    bits = [1 << k for k in range(parts.bit_length() - 1)]
    rest = bits[1:]
    cut = len(rest) // 2
    return bits[:1] + rest[:cut] + rest[cut:], bits[:1] + rest[cut:] + rest[:cut]


def greet(n, parts):
    ex, dp = lax.axis_index("expert"), lax.axis_index("dp")
    barrier = pltpu.get_barrier_semaphore()
    masks = list(range(1, n // 2 + 1))
    for d in masks:
        pl.semaphore_signal(barrier, inc=1, device_id={"expert": flip(ex, d)}, device_id_type=pl.DeviceIdType.MESH)
    bits = bit_orders(parts)[0]
    for b in bits:
        pl.semaphore_signal(barrier, inc=1, device_id={"dp": flip(dp, b)}, device_id_type=pl.DeviceIdType.MESH)
    pl.semaphore_wait(barrier, len(masks) + len(bits))
    return ex, dp


class Sender:
    def __init__(self, send, recv):
        self.send, self.recv, self.count, self.all = send, recv, 0, []

    def start(self, src, dst, axis, target):
        k = self.count
        self.count += 1
        copy = pltpu.make_async_remote_copy(
            src_ref=src, dst_ref=dst, send_sem=self.send.at[k], recv_sem=self.recv.at[k],
            device_id={axis: target}, device_id_type=pl.DeviceIdType.MESH,
        )
        copy.start()
        self.all.append(copy)
        return copy

    def drain(self):
        for copy in self.all:
            copy.wait_send()


def dispatch_kernel(n, parts, x, c, t, up, down, dec, xo, co, to, upo, downo, deco, send, recv):
    ex, dp = greet(n, parts)
    half = n // 2
    s = Sender(send, recv)
    mate = flip(ex, half)
    first_up = s.start(up.at[dp], upo.at[dp], "expert", mate)
    first_down = s.start(down.at[dp], downo.at[dp], "expert", mate)
    late = [s.start(dec, deco, "expert", mate)]
    for d in range(1, half):
        to_dev = flip(ex, d)
        late.append(s.start(t, to.at[d - 1], "expert", to_dev))
        late.append(s.start(x, xo.at[d - 1], "expert", to_dev))
        late.append(s.start(c, co.at[d - 1], "expert", to_dev))
    orders = [o[::-1] for o in bit_orders(parts)]
    waiting = [[first_up], [first_down]]
    held = [[0], [0]]
    for stage in range(len(orders[0])):
        for a, buf in ((0, upo), (1, downo)):
            for copy in waiting[a]:
                copy.wait_recv()
            b = orders[a][stage]
            waiting[a] = []
            for r in held[a]:
                place = flip(dp, r)
                waiting[a].append(s.start(buf.at[place], buf.at[place], "dp", flip(dp, b)))
            held[a] = held[a] + [r ^ b for r in held[a]]
    for copy in waiting[0] + waiting[1] + late:
        copy.wait_recv()
    s.drain()


def dispatch(n, parts, x, c, t, up, down, dec):
    half = n // 2
    stack = lambda v: jax.ShapeDtypeStruct((half - 1,) + v.shape, v.dtype)
    same = lambda v: jax.ShapeDtypeStruct(v.shape, v.dtype)
    copies = 3 + 3 * (half - 1) + 2 * (parts - 1)
    anywhere = pl.BlockSpec(memory_space=pl.ANY)
    return pl.pallas_call(
        partial(dispatch_kernel, n, parts),
        out_shape=(stack(x), stack(c), stack(t), same(up), same(down), same(dec)),
        in_specs=[anywhere] * 6,
        out_specs=[anywhere] * 6,
        scratch_shapes=[pltpu.SemaphoreType.DMA((copies,)), pltpu.SemaphoreType.DMA((copies,))],
        compiler_params=pltpu.CompilerParams(collective_id=0, has_side_effects=True),
        name="dispatch",
    )(x, c, t, up, down, dec)


def add_rows(rows, read_a, read_b, write):
    step = 32 if rows % 32 == 0 else rows

    @pl.loop(0, rows // step)
    def _(i):
        cut = pl.ds(pl.multiple_of(i * step, step), step)
        write(cut, read_a(cut).astype(F32) + read_b(cut).astype(F32))


def return_kernel(n, parts, up1, down1, up2, down2, lay, bak, dots, upo, downo, layo, bako, dotso,
                  slots, far, send, recv):
    ex, dp = greet(n, parts)
    half = n // 2
    s = Sender(send, recv)
    rows = up1.shape[1]
    grads = (up1, down1, up2, down2)
    orders = bit_orders(parts)
    orders = (orders[0], orders[1], orders[0], orders[1])
    stages = len(orders[0])
    place, keep = [], []
    for a in range(4):
        ids, kept, live, k = {}, [], list(range(parts)), 0
        for st in range(stages):
            live = [r for r in live if not r & orders[a][st]]
            kept.append(live)
            for r in live:
                ids[(st, r)] = k
                k += 1
        place.append(ids)
        keep.append(kept)

    def begin(a, st):
        b = orders[a][st]
        out = []
        for r in keep[a][st]:
            far_r = r ^ b
            src = grads[a].at[flip(dp, far_r)] if st == 0 else slots.at[a, place[a][(st - 1, far_r)]]
            out.append(s.start(src, slots.at[a, place[a][(st, r)]], "dp", flip(dp, b)))
        return out

    def finish(a, st, copies):
        for copy in copies:
            copy.wait_recv()
        for r in keep[a][st]:
            k = place[a][(st, r)]
            if st == 0:
                chunk = flip(dp, r)
                other = lambda cut: grads[a][chunk, cut, :]
            else:
                old = place[a][(st - 1, r)]
                other = lambda cut: slots[a, old, cut, :]
            if st == stages - 1 and a < 2:
                out = (upo, downo)[a]
                def write(cut, v):
                    out[cut, :] = v
            else:
                def write(cut, v):
                    slots[a, k, cut, :] = v.astype(BF)
            add_rows(rows, lambda cut: slots[a, k, cut, :], other, write)

    late = []
    run = {}
    for a in (2, 3, 0, 1):
        run[a] = begin(a, 0)
    for d in range(1, half):
        to_dev = flip(ex, d)
        late.append(s.start(lay.at[d - 1], layo.at[d - 1], "expert", to_dev))
        late.append(s.start(bak.at[d - 1], bako.at[d - 1], "expert", to_dev))
        late.append(s.start(dots.at[d - 1], dotso.at[d - 1], "expert", to_dev))
    swaps = []
    for st in range(stages):
        for a in (2, 3):
            finish(a, st, run[a])
            if st + 1 < stages:
                run[a] = begin(a, st + 1)
            else:
                k = place[a][(st, 0)]
                swaps.append(s.start(slots.at[a, k], far.at[a - 2], "expert", flip(ex, half)))
        if st > 0:
            for a in (0, 1):
                finish(a, st - 1, run[a])
                run[a] = begin(a, st)
    for a in (0, 1):
        finish(a, stages - 1, run[a])
    for a, out in ((0, upo), (1, downo)):
        swaps[a].wait_recv()

        def write(cut, v, out=out):
            out[cut, :] = v

        add_rows(rows, lambda cut: out[cut, :], lambda cut: far[a, cut, :], write)
    for copy in late:
        copy.wait_recv()
    s.drain()


def give_back(n, parts, grads, lay, bak, dots):
    half = n // 2
    same = lambda v: jax.ShapeDtypeStruct(v.shape, v.dtype)
    rows, cols = grads[0].shape[1:]
    copies = 4 * (parts - 1) + 2 + 3 * (half - 1)
    anywhere = pl.BlockSpec(memory_space=pl.ANY)
    vmem = pl.BlockSpec(memory_space=pltpu.VMEM)
    shard = jax.ShapeDtypeStruct((rows, cols), F32)
    return pl.pallas_call(
        partial(return_kernel, n, parts),
        out_shape=(shard, shard, same(lay), same(bak), same(dots)),
        in_specs=[vmem] * 4 + [anywhere] * 3,
        out_specs=[vmem] * 2 + [anywhere] * 3,
        scratch_shapes=[
            pltpu.VMEM((4, parts - 1, rows, cols), BF),
            pltpu.VMEM((2, rows, cols), BF),
            pltpu.SemaphoreType.DMA((copies,)),
            pltpu.SemaphoreType.DMA((copies,)),
        ],
        compiler_params=pltpu.CompilerParams(
            collective_id=1, has_side_effects=True, vmem_limit_bytes=50 * 2**20
        ),
        name="give_back",
    )(*grads, lay, bak, dots)


def local(tokens, cotangent, routes, gate_probs, w_up, w_down, decay_rate):
    rows, width = tokens.shape
    n = lax.axis_size("expert")
    parts = lax.axis_size("dp")
    half = n // 2
    me = lax.axis_index("expert")
    w_up, w_down, decay = w_up[0], w_down[0], decay_rate[0]
    hidden = w_up.shape[1]
    ids = jnp.arange(n, dtype=jnp.int32)
    hit = routes[None, :, :] == ids[:, None, None]
    table = jnp.sum(jnp.where(hit, gate_probs[None, :, :], 0.0), axis=2)
    x_far, cot_far, tab_far, w_up2, w_down2, decay2 = dispatch(
        n, parts, tokens, cotangent, table,
        w_up.reshape(parts, width // parts, hidden),
        w_down.reshape(parts, hidden // parts, width),
        decay[None],
    )
    w_up2 = w_up2.reshape(width, hidden)
    w_down2 = w_down2.reshape(hidden, width)
    decay2 = decay2[0]
    x_all = jnp.concatenate([tokens, x_far.reshape(-1, width)], axis=0)
    cot_all = jnp.concatenate([cotangent, cot_far.reshape(-1, width)], axis=0)
    tabs = jnp.concatenate([table[None], tab_far], axis=0)
    other = me ^ half

    def gate_of(expert):
        pick = (ids == expert)[None, :, None]
        return jnp.sum(jnp.where(pick, tabs, 0.0), axis=1).reshape(-1)

    def grad(a, b):
        return mm(a, b, ((0,), (0,))).astype(BF).reshape(parts, width // parts, hidden)

    layer1, dots1, back1, rates1, scaled1, cg1 = expert_block(
        x_all, cot_all, gate_of(me), w_up, w_down, decay
    )
    layer2, dots2, back2, rates2, scaled2, cg2 = expert_block(
        x_all, cot_all, gate_of(other), w_up2, w_down2, decay2
    )
    grads = (grad(x_all, cg1), grad(scaled1, rates1), grad(x_all, cg2), grad(scaled2, rates2))
    layer = (layer1 + layer2).reshape(half, rows, width)
    back = (back1 + back2).reshape(half, rows, width)
    dots = jnp.where((ids == me)[None, :, None], dots1.reshape(half, 1, rows), 0.0) + jnp.where(
        (ids == other)[None, :, None], dots2.reshape(half, 1, rows), 0.0
    )
    up_grad, down_grad, layer_far, back_far, dots_far = give_back(
        n, parts, grads, layer[1:].astype(BF), back[1:].astype(BF), dots[1:]
    )
    layer_out = layer[0] + jnp.sum(layer_far.astype(F32), axis=0)
    token_grad = back[0] + jnp.sum(back_far.astype(F32), axis=0)
    own = dots[0] + jnp.sum(dots_far, axis=0)
    gate_grad = jnp.sum(jnp.where(hit, own[:, :, None], 0.0), axis=0)
    return (layer_out.astype(BF), token_grad.astype(BF), gate_grad, up_grad[None], down_grad.T[None])


def solution(mesh):
    rows = P(("dp", "expert"), None)
    return jax.shard_map(
        local,
        mesh=mesh,
        in_specs=(rows, rows, rows, rows, P("expert", None, None), P("expert", None, None), P("expert", None)),
        out_specs=(rows, rows, rows, P("expert", "dp", None), P("expert", None, "dp")),
        check_vma=False,
    )
```

```python
from functools import partial

import jax
import jax.numpy as jnp
from jax import lax
from jax.experimental import pallas as pl
from jax.experimental.pallas import tpu as pltpu
from jax.sharding import PartitionSpec as P

STEPS = 4
SHARP = 4.0

BF = jnp.bfloat16
F32 = jnp.float32


def rate_and_slope(current, decay):
    v = jnp.zeros_like(current)
    dv = jnp.zeros_like(current)
    total = jnp.zeros_like(current)
    slope = jnp.zeros_like(current)
    for _ in range(STEPS):
        v = decay * v + current
        dv = decay * dv + 1.0
        s = jax.nn.sigmoid(SHARP * (v - 1.0))
        ds = SHARP * s * (1.0 - s) * dv
        v = v - s
        dv = dv - ds
        total = total + s
        slope = slope + ds
    return total / STEPS, slope / STEPS


def mm(a, b, dims):
    return lax.dot_general(a, b, (dims, ((), ())), preferred_element_type=F32)


def expert_block(x, cot, gate, w_up, w_down, decay):
    rates, slope = rate_and_slope(mm(x, w_up, ((1,), (0,))), decay)
    rates = rates.astype(BF)
    cot32 = cot.astype(F32)
    scaled = (gate[:, None] * cot32).astype(BF)
    out = mm(rates, w_down, ((1,), (0,))).astype(BF).astype(F32)
    layer = gate[:, None] * out
    dots = jnp.sum(cot32 * out, axis=1)
    rate_grad = mm(scaled, w_down, ((1,), (1,)))
    current_grad = (rate_grad * slope).astype(BF)
    back = mm(current_grad, w_up, ((1,), (1,))).astype(BF).astype(F32)
    return layer, dots, back, rates, scaled, current_grad


def flip(pos, mask):
    for k in range(mask.bit_length()):
        b = 1 << k
        if mask & b:
            pos = pos + b * (1 - 2 * ((pos // b) % 2))
    return pos


def bit_orders(parts):
    bits = [1 << k for k in range(parts.bit_length() - 1)]
    rest = bits[1:]
    cut = len(rest) // 2
    return bits[:1] + rest[:cut] + rest[cut:], bits[:1] + rest[cut:] + rest[:cut]


def greet(n, parts):
    ex, dp = lax.axis_index("expert"), lax.axis_index("dp")
    barrier = pltpu.get_barrier_semaphore()
    masks = list(range(1, n // 2 + 1))
    for d in masks:
        pl.semaphore_signal(barrier, inc=1, device_id={"expert": flip(ex, d)}, device_id_type=pl.DeviceIdType.MESH)
    bits = bit_orders(parts)[0]
    for b in bits:
        pl.semaphore_signal(barrier, inc=1, device_id={"dp": flip(dp, b)}, device_id_type=pl.DeviceIdType.MESH)
    pl.semaphore_wait(barrier, len(masks) + len(bits))
    return ex, dp


class Sender:
    def __init__(self, send, recv):
        self.send, self.recv, self.count, self.all = send, recv, 0, []

    def start(self, src, dst, axis, target):
        k = self.count
        self.count += 1
        copy = pltpu.make_async_remote_copy(
            src_ref=src, dst_ref=dst, send_sem=self.send.at[k], recv_sem=self.recv.at[k],
            device_id={axis: target}, device_id_type=pl.DeviceIdType.MESH,
        )
        copy.start()
        self.all.append(copy)
        return copy

    def drain(self):
        for copy in self.all:
            copy.wait_send()


def dispatch_kernel(n, parts, x, c, t, up, down, dec, xo, co, to, upo, downo, deco, send, recv):
    ex, dp = greet(n, parts)
    half = n // 2
    s = Sender(send, recv)
    mate = flip(ex, half)
    first_up = s.start(up.at[dp], upo.at[dp], "expert", mate)
    first_down = s.start(down.at[dp], downo.at[dp], "expert", mate)
    late = [s.start(dec, deco, "expert", mate)]
    for d in range(1, half):
        to_dev = flip(ex, d)
        late.append(s.start(t, to.at[d - 1], "expert", to_dev))
        late.append(s.start(x, xo.at[d - 1], "expert", to_dev))
        late.append(s.start(c, co.at[d - 1], "expert", to_dev))
    orders = [o[::-1] for o in bit_orders(parts)]
    waiting = [[first_up], [first_down]]
    held = [[0], [0]]
    for stage in range(len(orders[0])):
        for a, buf in ((0, upo), (1, downo)):
            for copy in waiting[a]:
                copy.wait_recv()
            b = orders[a][stage]
            waiting[a] = []
            for r in held[a]:
                place = flip(dp, r)
                waiting[a].append(s.start(buf.at[place], buf.at[place], "dp", flip(dp, b)))
            held[a] = held[a] + [r ^ b for r in held[a]]
    for copy in waiting[0] + waiting[1] + late:
        copy.wait_recv()
    s.drain()


def dispatch(n, parts, x, c, t, up, down, dec):
    half = n // 2
    stack = lambda v: jax.ShapeDtypeStruct((half - 1,) + v.shape, v.dtype)
    same = lambda v: jax.ShapeDtypeStruct(v.shape, v.dtype)
    copies = 3 + 3 * (half - 1) + 2 * (parts - 1)
    anywhere = pl.BlockSpec(memory_space=pl.ANY)
    return pl.pallas_call(
        partial(dispatch_kernel, n, parts),
        out_shape=(stack(x), stack(c), stack(t), same(up), same(down), same(dec)),
        in_specs=[anywhere] * 6,
        out_specs=[anywhere] * 6,
        scratch_shapes=[pltpu.SemaphoreType.DMA((copies,)), pltpu.SemaphoreType.DMA((copies,))],
        compiler_params=pltpu.CompilerParams(collective_id=0, has_side_effects=True),
        name="dispatch",
    )(x, c, t, up, down, dec)


def add_rows(rows, read_a, read_b, write):
    step = 32 if rows % 32 == 0 else rows

    @pl.loop(0, rows // step)
    def _(i):
        cut = pl.ds(pl.multiple_of(i * step, step), step)
        write(cut, read_a(cut).astype(F32) + read_b(cut).astype(F32))


def return_kernel(n, parts, x, cg1, sc1, rt1, cg2, sc2, rt2, lay, bak, dots, upo, downo, layo, bako,
                  dotso, products, slots, far, send, recv):
    ex, dp = greet(n, parts)
    half = n // 2
    s = Sender(send, recv)
    rows = slots.shape[2]
    grads = [products.at[a] for a in range(4)]
    pairs = ((x, cg1), (sc1, rt1), (x, cg2), (sc2, rt2))
    tile = 256
    per = tile // rows

    def multiply(a):
        left, right = pairs[a]

        @pl.loop(0, left.shape[1] // tile)
        def _(i):
            cols = pl.ds(pl.multiple_of(i * tile, tile), tile)
            res = mm(left[:, cols], right[...], ((0,), (0,))).astype(BF)
            for k in range(per):
                products[a, i * per + k] = res[k * rows:(k + 1) * rows]

    orders = bit_orders(parts)
    orders = (orders[0], orders[1], orders[0], orders[1])
    stages = len(orders[0])
    place, keep = [], []
    for a in range(4):
        ids, kept, live, k = {}, [], list(range(parts)), 0
        for st in range(stages):
            live = [r for r in live if not r & orders[a][st]]
            kept.append(live)
            for r in live:
                ids[(st, r)] = k
                k += 1
        place.append(ids)
        keep.append(kept)

    def begin(a, st):
        b = orders[a][st]
        out = []
        for r in keep[a][st]:
            far_r = r ^ b
            src = grads[a].at[flip(dp, far_r)] if st == 0 else slots.at[a, place[a][(st - 1, far_r)]]
            out.append(s.start(src, slots.at[a, place[a][(st, r)]], "dp", flip(dp, b)))
        return out

    def finish(a, st, copies):
        for copy in copies:
            copy.wait_recv()
        for r in keep[a][st]:
            k = place[a][(st, r)]
            if st == 0:
                chunk = flip(dp, r)
                other = lambda cut: products[a, chunk, cut, :]
            else:
                old = place[a][(st - 1, r)]
                other = lambda cut: slots[a, old, cut, :]
            if st == stages - 1 and a < 2:
                out = (upo, downo)[a]
                def write(cut, v):
                    out[cut, :] = v
            else:
                def write(cut, v):
                    slots[a, k, cut, :] = v.astype(BF)
            add_rows(rows, lambda cut: slots[a, k, cut, :], other, write)

    late = []
    run = {}
    for d in range(1, half):
        to_dev = flip(ex, d)
        late.append(s.start(lay.at[d - 1], layo.at[d - 1], "expert", to_dev))
        late.append(s.start(bak.at[d - 1], bako.at[d - 1], "expert", to_dev))
        late.append(s.start(dots.at[d - 1], dotso.at[d - 1], "expert", to_dev))
    for a in (2, 3):
        multiply(a)
        run[a] = begin(a, 0)
    swaps = []
    for st in range(stages):
        for a in (2, 3):
            finish(a, st, run[a])
            if st + 1 < stages:
                run[a] = begin(a, st + 1)
            else:
                k = place[a][(st, 0)]
                swaps.append(s.start(slots.at[a, k], far.at[a - 2], "expert", flip(ex, half)))
        for a in (0, 1):
            if st == 0:
                multiply(a)
                run[a] = begin(a, 0)
            else:
                finish(a, st - 1, run[a])
                run[a] = begin(a, st)
    for a in (0, 1):
        finish(a, stages - 1, run[a])
    for a, out in ((0, upo), (1, downo)):
        swaps[a].wait_recv()

        def write(cut, v, out=out):
            out[cut, :] = v

        add_rows(rows, lambda cut: out[cut, :], lambda cut: far[a, cut, :], write)
    for copy in late:
        copy.wait_recv()
    s.drain()


def give_back(n, parts, factors, lay, bak, dots):
    half = n // 2
    same = lambda v: jax.ShapeDtypeStruct(v.shape, v.dtype)
    rows, cols = factors[0].shape[1] // parts, factors[1].shape[1]
    copies = 4 * (parts - 1) + 2 + 3 * (half - 1)
    anywhere = pl.BlockSpec(memory_space=pl.ANY)
    vmem = pl.BlockSpec(memory_space=pltpu.VMEM)
    shard = jax.ShapeDtypeStruct((rows, cols), F32)
    return pl.pallas_call(
        partial(return_kernel, n, parts),
        out_shape=(shard, shard, same(lay), same(bak), same(dots)),
        in_specs=[vmem] * 7 + [anywhere] * 3,
        out_specs=[vmem] * 2 + [anywhere] * 3,
        scratch_shapes=[
            pltpu.VMEM((4, parts, rows, cols), BF),
            pltpu.VMEM((4, parts - 1, rows, cols), BF),
            pltpu.VMEM((2, rows, cols), BF),
            pltpu.SemaphoreType.DMA((copies,)),
            pltpu.SemaphoreType.DMA((copies,)),
        ],
        compiler_params=pltpu.CompilerParams(
            collective_id=1, has_side_effects=True, vmem_limit_bytes=50 * 2**20
        ),
        name="give_back",
    )(*factors, lay, bak, dots)


def local(tokens, cotangent, routes, gate_probs, w_up, w_down, decay_rate):
    rows, width = tokens.shape
    n = lax.axis_size("expert")
    parts = lax.axis_size("dp")
    half = n // 2
    me = lax.axis_index("expert")
    w_up, w_down, decay = w_up[0], w_down[0], decay_rate[0]
    hidden = w_up.shape[1]
    ids = jnp.arange(n, dtype=jnp.int32)
    hit = routes[None, :, :] == ids[:, None, None]
    table = jnp.sum(jnp.where(hit, gate_probs[None, :, :], 0.0), axis=2)
    x_far, cot_far, tab_far, w_up2, w_down2, decay2 = dispatch(
        n, parts, tokens, cotangent, table,
        w_up.reshape(parts, width // parts, hidden),
        w_down.reshape(parts, hidden // parts, width),
        decay[None],
    )
    w_up2 = w_up2.reshape(width, hidden)
    w_down2 = w_down2.reshape(hidden, width)
    decay2 = decay2[0]
    x_all = jnp.concatenate([tokens, x_far.reshape(-1, width)], axis=0)
    cot_all = jnp.concatenate([cotangent, cot_far.reshape(-1, width)], axis=0)
    tabs = jnp.concatenate([table[None], tab_far], axis=0)
    other = me ^ half

    def gate_of(expert):
        pick = (ids == expert)[None, :, None]
        return jnp.sum(jnp.where(pick, tabs, 0.0), axis=1).reshape(-1)

    layer1, dots1, back1, rates1, scaled1, cg1 = expert_block(
        x_all, cot_all, gate_of(me), w_up, w_down, decay
    )
    layer2, dots2, back2, rates2, scaled2, cg2 = expert_block(
        x_all, cot_all, gate_of(other), w_up2, w_down2, decay2
    )
    factors = (x_all, cg1, scaled1, rates1, cg2, scaled2, rates2)
    layer = (layer1 + layer2).reshape(half, rows, width)
    back = (back1 + back2).reshape(half, rows, width)
    dots = jnp.where((ids == me)[None, :, None], dots1.reshape(half, 1, rows), 0.0) + jnp.where(
        (ids == other)[None, :, None], dots2.reshape(half, 1, rows), 0.0
    )
    up_grad, down_grad, layer_far, back_far, dots_far = give_back(
        n, parts, factors, layer[1:].astype(BF), back[1:].astype(BF), dots[1:]
    )
    layer_out = layer[0] + jnp.sum(layer_far.astype(F32), axis=0)
    token_grad = back[0] + jnp.sum(back_far.astype(F32), axis=0)
    own = dots[0] + jnp.sum(dots_far, axis=0)
    gate_grad = jnp.sum(jnp.where(hit, own[:, :, None], 0.0), axis=0)
    return (layer_out.astype(BF), token_grad.astype(BF), gate_grad, up_grad[None], down_grad.T[None])


def solution(mesh):
    rows = P(("dp", "expert"), None)
    return jax.shard_map(
        local,
        mesh=mesh,
        in_specs=(rows, rows, rows, rows, P("expert", None, None), P("expert", None, None), P("expert", None)),
        out_specs=(rows, rows, rows, P("expert", "dp", None), P("expert", None, "dp")),
        check_vma=False,
    )
```
